32 devices in a mesh: groups: 2 (over x), tensor: 8 (over z, y), seq: 2 (over core).
Axes of the slice: x: 2, y: 2, z: 4, core: 2. Of those that a mesh axis runs over, the one named last changes fastest.
Arguments:
- heads_out: bfloat16 [128, 4096], P(('groups', 'seq'), 'tensor'), parts along dimension 0, may hold values from -6 to 6
- stream_in: bfloat16 [128, 8192], P(('groups', 'seq', 'tensor')), parts along dimension 0, may hold values from -40 to 40, as said below
- proj_levels: bfloat16 [4096, 8192], P('tensor'), may hold values from -8 to 7, as said below
- proj_scale: float32 [8192], replicated, may hold values from 0.001703125 to 0.006796875
- norm_gain: float32 [8192], replicated, may hold values from 0.25 to 1.75
- gate_levels: bfloat16 [8192, 14336], P(None, 'tensor'), may hold values from -8 to 7, as said below
- gate_scale: float32 [14336], P('tensor'), may hold values from 0.0012153398 to 0.004861359
- gate_index: int32 [8, 8], P('tensor'), may hold values from 0 to 1791, as said below
- gate_extra: bfloat16 [8192, 64], P(None, 'tensor'), may hold values from -0.29882812 to 0.29882812
- up_levels: bfloat16 [8192, 14336], P(None, 'tensor'), may hold values from -8 to 7, as said below
- up_scale: float32 [14336], P('tensor'), may hold values from 0.0012153398 to 0.004861359
- up_index: int32 [8, 8], P('tensor'), may hold values from 0 to 1791, as said below
- up_extra: bfloat16 [8192, 64], P(None, 'tensor'), may hold values from -0.29882812 to 0.29882812
- down_levels: bfloat16 [14336, 8192], P('tensor'), may hold values from -8 to 7, as said below
- down_scale: float32 [8192], replicated, may hold values from 0.0009020067 to 0.003591323
- down_index: int32 [8, 8], P('tensor'), may hold values from 0 to 8191, as said below
- down_extra: bfloat16 [14336, 8], P('tensor'), may hold values from -0.29882812 to 0.29882812
Outputs:
- stream_out: bfloat16 [128, 8192], P(('groups', 'seq', 'tensor')), parts along dimension 0
The draws below stay inside these ranges and needn't reach their ends.
There are 2 independent parts, one for each index of `groups`. The reference program is written for one: setup_inputs(seed, part) draws one part's arguments, and reference() takes and returns one part's arrays. A program takes and returns all parts, laid end to end along the dimension named above; an argument that names none is the same for every part. Nothing has to cross between parts.
Inputs may be any that keep to these rules, and one draw needn't show every extreme that they name: stream_in has rows and columns of differing scales. `proj_levels`: integer values. `gate_levels`: integer values. `up_levels`: integer values. `down_levels`: integer values. `gate_index`: each row holds 8 different numbers. `up_index`: each row holds 8 different numbers. `down_index`: each row holds 8 different numbers.
All inputs are finite; a program needn't handle non-finite values.
Results may differ from the reference program's by a relative error of at most 0.0055.
Values may be sent and summed in bfloat16 or wider, within the bound.
No kernel may reach another device: no remote copies, remote signals or barrier semaphores. Data moves between devices by JAX's collectives and lax.ppermute only.
A program may use at most 192 MiB of HBM per device.

```python
import math
import jax
import jax.numpy as jnp
from jax import lax

D = 8192
HD = 4096
FF = 14336
K_OUT = 8
TOKENS = 64
N_TENSOR = 8


def level_draw(key, rows, columns):
    return jax.random.randint(key, (rows, columns), -8, 8).astype(jnp.float32)


def index_draw(key, width):
    row_key, edge_key, inner_key = jax.random.split(key, 3)
    keys = jax.random.split(row_key, N_TENSOR)
    orders = jax.vmap(lambda single: jax.random.permutation(single, width))(keys)[:, :K_OUT].astype(jnp.int32)
    inner = (jax.random.permutation(inner_key, width - 2) + 1).astype(jnp.int32)
    edge_row = jnp.concatenate([jnp.array([0, width - 1], dtype=jnp.int32), inner[:K_OUT - 2]])
    chosen = jax.random.randint(edge_key, (), 0, N_TENSOR)
    rows = jnp.arange(N_TENSOR, dtype=jnp.int32)[:, None]
    return jnp.where(rows == chosen, edge_row[None, :], orders).astype(jnp.int32)


def draw_proj_levels(key, part):
    return level_draw(jax.random.fold_in(key, 11), HD, D).astype(jnp.bfloat16)


def draw_gate_levels(key, part):
    return level_draw(jax.random.fold_in(key, 12), D, FF).astype(jnp.bfloat16)


def draw_up_levels(key, part):
    return level_draw(jax.random.fold_in(key, 13), D, FF).astype(jnp.bfloat16)


def draw_down_levels(key, part):
    return level_draw(jax.random.fold_in(key, 14), FF, D).astype(jnp.bfloat16)


def draw_gate_index(key, part):
    return index_draw(jax.random.fold_in(key, 21), FF // N_TENSOR)


def draw_up_index(key, part):
    return index_draw(jax.random.fold_in(key, 22), FF // N_TENSOR)


def draw_down_index(key, part):
    return index_draw(jax.random.fold_in(key, 23), D)


def draw_stream_in(key, part):
    row_key, col_key, base_key = jax.random.split(jax.random.fold_in(key, 31), 3)
    row_scale = jnp.exp(jax.random.uniform(row_key, (TOKENS, 1), jnp.float32, jnp.log(0.3), jnp.log(3.0)))
    col_scale = jnp.exp(jax.random.uniform(col_key, (1, D), jnp.float32, jnp.log(0.3), jnp.log(3.0)))
    base = jnp.clip(jax.random.normal(base_key, (TOKENS, D), jnp.float32), -4.0, 4.0)
    return (base * row_scale * col_scale).astype(jnp.bfloat16)


def level_of(own_key, shape, pieces, low, high):
    loudness = 1.0
    for dim, blocks in pieces:
        draws = jax.random.uniform(jax.random.fold_in(jax.random.fold_in(own_key, 6), dim), (blocks,), jnp.float32, low / len(pieces), high / len(pieces))
        loudness = loudness * jnp.repeat(jnp.exp(draws), shape[dim] // blocks).reshape((-1,) + (1,) * (len(shape) - 1 - dim))
    return loudness


def noise(own_key, dims, spread, most, cuts=(), kind=jnp.bfloat16):
    values = spread * jax.random.normal(own_key, dims, jnp.float32)
    if cuts:
        values = values * level_of(own_key, dims, cuts, -0.22, 0.18)
    return jnp.clip(values, -most, most).astype(kind)


def setup_inputs(seed: int = 0, part: int = 0) -> dict:
    key_list = jax.random.split(jax.random.key(seed), 18)
    part_splits = jax.random.split(jax.random.fold_in(key_list[17], part), 18)
    return {
        "heads_out": noise(part_splits[0], (TOKENS, HD), 1.0, 6.0, ((0, 2), (1, 8))),
        "stream_in": draw_stream_in(jax.random.fold_in(jax.random.fold_in(key_list[17], part), 71), part),
        "proj_levels": draw_proj_levels(jax.random.fold_in(key_list[17], 71), part),
        "proj_scale": jnp.clip(jnp.exp(jax.random.uniform(key_list[3], (D,), jnp.float32, math.log(0.001703125), math.log(0.006796875))), 0.001703125, 0.006796875),
        "norm_gain": jnp.clip(1.0 + 0.15 * jax.random.normal(key_list[4], (D,), jnp.float32), 0.25, 1.75),
        "gate_levels": draw_gate_levels(jax.random.fold_in(key_list[17], 71), part),
        "gate_scale": jnp.clip(jnp.exp(math.log(0.004861359) - 1.3862944 * jax.random.uniform(key_list[6], (FF,), jnp.float32) ** level_of(key_list[6], (FF,), ((0, 8),), -0.2, 0.2)), 0.0012153398, 0.004861359),
        "gate_index": draw_gate_index(jax.random.fold_in(key_list[17], 71), part),
        "gate_extra": noise(key_list[8], (D, N_TENSOR * K_OUT), 0.05, 0.29882812, ((1, 8),)),
        "up_levels": draw_up_levels(jax.random.fold_in(key_list[17], 71), part),
        "up_scale": jnp.clip(jnp.exp(math.log(0.004861359) - 1.3862944 * jax.random.uniform(key_list[10], (FF,), jnp.float32) ** level_of(key_list[10], (FF,), ((0, 8),), -0.2, 0.2)), 0.0012153398, 0.004861359),
        "up_index": draw_up_index(jax.random.fold_in(key_list[17], 71), part),
        "up_extra": noise(key_list[12], (D, N_TENSOR * K_OUT), 0.05, 0.29882812, ((1, 8),)),
        "down_levels": draw_down_levels(jax.random.fold_in(key_list[17], 71), part),
        "down_scale": jnp.clip(jnp.exp(jax.random.uniform(key_list[14], (D,), jnp.float32, math.log(0.0009020067), math.log(0.003591323))), 0.0009020067, 0.003591323),
        "down_index": draw_down_index(jax.random.fold_in(key_list[17], 71), part),
        "down_extra": noise(key_list[16], (FF, K_OUT), 0.05, 0.29882812, ((0, 8),)),
    }


def wide_dot(left, right):
    return jnp.dot(left.astype(jnp.float32), right.astype(jnp.float32), precision=lax.Precision.HIGHEST, preferred_element_type=jnp.float32)

def rms_norm(mixed, norm_gain):
    mean_sq = lax.optimization_barrier(jnp.mean(mixed * mixed, axis=-1, keepdims=True))
    return (mixed * lax.rsqrt(mean_sq + 1e-05) * norm_gain).astype(jnp.bfloat16)

def column_parallel(normed, levels, scale, index, extra):
    shard_width = FF // N_TENSOR
    base = wide_dot(normed, levels) * scale
    added = wide_dot(normed, extra)
    columns = (jnp.arange(N_TENSOR, dtype=jnp.int32)[:, None] * shard_width + index.astype(jnp.int32)).reshape(-1).astype(jnp.int32)
    return base.at[:, columns].add(added)

def reference(heads_out, stream_in, proj_levels, proj_scale, norm_gain, gate_levels, gate_scale, gate_index, gate_extra, up_levels, up_scale, up_index, up_extra, down_levels, down_scale, down_index, down_extra):
    shard_width = FF // N_TENSOR
    proj = wide_dot(heads_out, proj_levels) * proj_scale
    mixed = stream_in.astype(jnp.float32) + proj
    normed = rms_norm(mixed, norm_gain)
    gate = column_parallel(normed, gate_levels, gate_scale, gate_index, gate_extra)
    up = column_parallel(normed, up_levels, up_scale, up_index, up_extra)
    hidden = (jax.nn.silu(gate) * up).astype(jnp.bfloat16)
    down = wide_dot(hidden, down_levels) * down_scale
    parts = hidden.astype(jnp.float32).reshape(hidden.shape[0], N_TENSOR, shard_width)
    extra = down_extra.astype(jnp.float32).reshape(N_TENSOR, shard_width, K_OUT)
    added = jnp.einsum('tns,nsk->tnk', parts, extra, precision=lax.Precision.HIGHEST).reshape(hidden.shape[0], N_TENSOR * K_OUT)
    down = down.at[:, down_index.reshape(-1).astype(jnp.int32)].add(added)
    return (mixed + down).astype(jnp.bfloat16)
```

```python
import jax
import jax.numpy as jnp
from jax import lax
from jax.experimental import pallas as pl
from jax.experimental.pallas import tpu as pltpu
from jax.sharding import PartitionSpec as P


VMEM = pl.BlockSpec(memory_space=pltpu.VMEM)
SMEM = pl.BlockSpec(memory_space=pltpu.SMEM)
HBM = pl.BlockSpec(memory_space=pl.ANY)
EPS = 1e-05
LANES = 128


def params(mib):
    return pltpu.CompilerParams(vmem_limit_bytes=mib * 1024 * 1024)


def whole_parts(size, want):
    for count in range(want, 0, -1):
        if size % (count * LANES) == 0:
            return count
    return 1


def proj_kernel(rows, parts, me_ref, heads_ref, levels_hbm, scale_ref, *refs):
    outs, (held, sems) = refs[:-2], refs[-2:]
    pieces = len(outs)
    width = levels_hbm.shape[1] // parts

    def copy(i):
        return pltpu.make_async_copy(
            levels_hbm.at[:, pl.ds(i * width, width)], held.at[i], sems.at[i]
        )

    for i in range(parts):
        copy(i).start()
    me = me_ref[0]
    tokens = pieces * rows
    line = lax.broadcasted_iota(jnp.int32, (tokens, tokens), 0)
    source = jnp.bitwise_xor(lax.div(line, rows), me) * rows + lax.rem(line, rows)
    moved = lax.broadcasted_iota(jnp.int32, (tokens, tokens), 1) == source
    lhs = jnp.dot(
        moved.astype(jnp.float32).astype(jnp.bfloat16), heads_ref[...], preferred_element_type=jnp.float32
    ).astype(jnp.bfloat16)
    for i in range(parts):
        copy(i).wait()
        cols = slice(i * width, (i + 1) * width)
        partial = jnp.dot(lhs, held[i], preferred_element_type=jnp.float32)
        partial = partial * scale_ref[:, cols]
        for k in range(pieces):
            outs[k][:, cols] = partial[k * rows : (k + 1) * rows, :].astype(outs[k].dtype)


def project_out(me, heads, levels, scale, rows, pieces):
    features, width = levels.shape
    parts = whole_parts(width, 8)
    shapes = [jax.ShapeDtypeStruct((rows, width), jnp.float32)]
    shapes += [jax.ShapeDtypeStruct((rows, width), jnp.bfloat16)] * (pieces - 1)

    def body(*refs):
        proj_kernel(rows, parts, *refs)

    return pl.pallas_call(
        body,
        name="project_out",
        out_shape=shapes,
        in_specs=[SMEM, VMEM, HBM, VMEM],
        out_specs=[VMEM] * pieces,
        scratch_shapes=[
            pltpu.VMEM((parts, features, width // parts), jnp.bfloat16),
            pltpu.SemaphoreType.DMA((parts,)),
        ],
        compiler_params=params(16),
    )(me, heads, levels, scale)


def norm_kernel(stream_ref, gain_ref, own_ref, *refs):
    others, (mixed_ref, normed_ref) = refs[:-2], refs[-2:]
    mixed = own_ref[...]
    for other in others:
        mixed = mixed + other[...].astype(jnp.float32)
    mixed = stream_ref[...].astype(jnp.float32) + mixed
    mixed_ref[...] = mixed
    mean_sq = jnp.mean(mixed * mixed, axis=-1, keepdims=True)
    normed_ref[...] = (mixed * lax.rsqrt(mean_sq + EPS) * gain_ref[...]).astype(jnp.bfloat16)


def mix_and_norm(stream, gain, own, others):
    return pl.pallas_call(
        norm_kernel,
        name="mix_and_norm",
        out_shape=[
            jax.ShapeDtypeStruct(own.shape, jnp.float32),
            jax.ShapeDtypeStruct(own.shape, jnp.bfloat16),
        ],
        in_specs=[VMEM] * (3 + len(others)),
        out_specs=[VMEM] * 2,
        compiler_params=params(8),
    )(stream, gain, own, *others)


def against(rows_in, extra):
    return lax.dot_general(
        rows_in, extra, (((1,), (1,)), ((), ())), preferred_element_type=jnp.float32
    )


def place(added, index_ref, first, width):
    count = added.shape[1]
    high = added.astype(jnp.bfloat16)
    low = (added - high.astype(jnp.float32)).astype(jnp.bfloat16)
    columns = lax.broadcasted_iota(jnp.int32, (count, width), 1) + first
    which = lax.broadcasted_iota(jnp.int32, (count, width), 0)
    target = jnp.full((count, width), -1, jnp.int32)
    for k in range(count):
        target = jnp.where(which == k, index_ref[0, k], target)
    chosen = (columns == target).astype(jnp.float32).astype(jnp.bfloat16)
    return jnp.dot(high, chosen, preferred_element_type=jnp.float32) + jnp.dot(
        low, chosen, preferred_element_type=jnp.float32
    )


def mlp_kernel(
    rows, depth, nbuf, parts,
    gate_scale, gate_index, gate_extra, up_scale, up_index, up_extra,
    down_scale, down_index, down_extra, gate_hbm, up_hbm, down_hbm, *refs,
):
    (stacked, x_ref, gate_acc, up_acc, ring, held, ring_sems, held_sems) = refs[-8:]
    refs = refs[:-8]
    pieces = len(refs) // 2
    ins, outs = refs[:pieces], refs[pieces:]
    width = down_hbm.shape[1] // parts
    steps = gate_hbm.shape[0] // depth

    def feed(i):
        source = (gate_hbm, up_hbm)[i % 2]
        return pltpu.make_async_copy(
            source.at[pl.ds((i // 2) * depth, depth), :], ring.at[i % nbuf], ring_sems.at[i % nbuf]
        )

    def feed_down(i):
        return pltpu.make_async_copy(
            down_hbm.at[:, pl.ds(i * width, width)], held.at[i], held_sems.at[i]
        )

    total = 2 * steps
    for i in range(min(nbuf, total)):
        feed(i).start()
    for k in range(pieces):
        stacked[k * rows : (k + 1) * rows, :] = ins[k][...].astype(jnp.float32)
    x_ref[...] = stacked[...].astype(jnp.bfloat16)
    sent = 0
    for i in range(total):
        feed(i).wait()
        acc = (gate_acc, up_acc)[i % 2]
        s = i // 2
        product = jnp.dot(
            x_ref[:, s * depth : (s + 1) * depth], ring[i % nbuf], preferred_element_type=jnp.float32
        )
        if s == 0:
            acc[...] = product
        else:
            acc[...] += product
        if i + nbuf < total:
            feed(i + nbuf).start()
        elif sent < parts:
            feed_down(sent).start()
            sent += 1
    while sent < parts:
        feed_down(sent).start()
        sent += 1
    x = x_ref[...]
    shard = gate_acc.shape[1]
    gate = gate_acc[...] * gate_scale[...] + place(against(x, gate_extra[...]), gate_index, 0, shard)
    up = up_acc[...] * up_scale[...] + place(against(x, up_extra[...]), up_index, 0, shard)
    hidden = (gate / (1.0 + jnp.exp(-gate)) * up).astype(jnp.bfloat16)
    added = against(hidden, down_extra[...])
    for i in range(parts):
        feed_down(i).wait()
        cols = slice(i * width, (i + 1) * width)
        partial = jnp.dot(hidden, held[i], preferred_element_type=jnp.float32)
        partial = partial * down_scale[:, cols] + place(added, down_index, i * width, width)
        for k in range(pieces):
            outs[k][:, cols] = partial[k * rows : (k + 1) * rows, :].astype(outs[k].dtype)


def mlp(normed, gate, up, down):
    gate_levels, gate_scale, gate_index, gate_extra = gate
    up_levels, up_scale, up_index, up_extra = up
    down_levels, down_scale, down_index, down_extra = down
    pieces, (rows, width) = len(normed), normed[0].shape
    shard = gate_levels.shape[1]
    tokens = pieces * rows
    depth = width // whole_parts(width, 8)
    parts = whole_parts(width, 8)
    nbuf = 7
    shapes = [jax.ShapeDtypeStruct((rows, width), jnp.float32)]
    shapes += [jax.ShapeDtypeStruct((rows, width), jnp.bfloat16)] * (pieces - 1)

    def body(*refs):
        mlp_kernel(rows, depth, nbuf, parts, *refs)

    return pl.pallas_call(
        body,
        name="mlp",
        out_shape=shapes,
        in_specs=[VMEM, SMEM, VMEM, VMEM, SMEM, VMEM, VMEM, SMEM, VMEM, HBM, HBM, HBM] + [VMEM] * pieces,
        out_specs=[VMEM] * pieces,
        scratch_shapes=[
            pltpu.VMEM((tokens, width), jnp.float32),
            pltpu.VMEM((tokens, width), jnp.bfloat16),
            pltpu.VMEM((tokens, shard), jnp.float32),
            pltpu.VMEM((tokens, shard), jnp.float32),
            pltpu.VMEM((nbuf, depth, shard), jnp.bfloat16),
            pltpu.VMEM((parts, shard, width // parts), jnp.bfloat16),
            pltpu.SemaphoreType.DMA((nbuf,)),
            pltpu.SemaphoreType.DMA((parts,)),
        ],
        compiler_params=params(60),
    )(
        gate_scale[None], gate_index, gate_extra.T, up_scale[None], up_index, up_extra.T,
        down_scale[None], down_index, down_extra.T, gate_levels, up_levels, down_levels, *normed,
    )


def finish_kernel(mixed_ref, own_ref, *refs):
    others, out_ref = refs[:-1], refs[-1]
    down = own_ref[...]
    for other in others:
        down = down + other[...].astype(jnp.float32)
    out_ref[...] = (mixed_ref[...] + down).astype(jnp.bfloat16)


def finish(mixed, own, others):
    return pl.pallas_call(
        finish_kernel,
        name="finish",
        out_shape=jax.ShapeDtypeStruct(own.shape, jnp.bfloat16),
        in_specs=[VMEM] * (2 + len(others)),
        out_specs=VMEM,
        compiler_params=params(8),
    )(mixed, own, *others)


def exchange(arrays, size):
    return [
        lax.ppermute(array, "tensor", [(i, i ^ k) for i in range(size)])
        for k, array in enumerate(arrays, 1)
    ]


def direct(
    size, heads_out, stream_in, proj_levels, proj_scale, norm_gain,
    gate_levels, gate_scale, gate_index, gate_extra,
    up_levels, up_scale, up_index, up_extra,
    down_levels, down_scale, down_index, down_extra,
):
    rows = stream_in.shape[0]
    me = lax.axis_index("tensor").astype(jnp.int32).reshape(1)
    own, *away = project_out(me, heads_out, proj_levels, proj_scale[None], rows, size)
    mixed, normed = mix_and_norm(stream_in, norm_gain[None], own, exchange(away, size))
    gathered = [normed] + exchange([normed] * (size - 1), size)
    own, *away = mlp(
        gathered,
        (gate_levels, gate_scale, gate_index, gate_extra),
        (up_levels, up_scale, up_index, up_extra),
        (down_levels, down_scale, down_index, down_extra),
    )
    return finish(mixed, own, exchange(away, size))


def rms_norm(mixed, norm_gain):
    mean_sq = jnp.mean(mixed * mixed, axis=-1, keepdims=True)
    return (mixed * lax.rsqrt(mean_sq + EPS) * norm_gain).astype(jnp.bfloat16)


def picker(index_row, width):
    return (index_row[:, None] == jnp.arange(width, dtype=jnp.int32)[None, :]).astype(jnp.float32)


def project(rows_in, levels, scale, extra, chosen):
    base = jnp.dot(rows_in, levels, preferred_element_type=jnp.float32)
    added = jnp.dot(rows_in, extra, preferred_element_type=jnp.float32)
    return base * scale + jnp.dot(added, chosen, precision=lax.Precision.HIGHEST)


def plain(
    heads_out, stream_in, proj_levels, proj_scale, norm_gain,
    gate_levels, gate_scale, gate_index, gate_extra,
    up_levels, up_scale, up_index, up_extra,
    down_levels, down_scale, down_index, down_extra,
):
    own_rows = stream_in.shape[0]
    shard_width = gate_levels.shape[1]
    model_width = proj_levels.shape[1]
    gate_pick = picker(gate_index[0], shard_width)
    up_pick = picker(up_index[0], shard_width)
    down_pick = picker(down_index[0], model_width)
    total = lax.psum(
        jnp.dot(heads_out, proj_levels, preferred_element_type=jnp.float32) * proj_scale, "tensor"
    )
    stream_all = lax.all_gather(stream_in, "tensor", axis=0, tiled=True)
    mixed_all = stream_all.astype(jnp.float32) + total
    normed_rows = rms_norm(mixed_all, norm_gain)
    gate = project(normed_rows, gate_levels, gate_scale, gate_extra, gate_pick)
    up = project(normed_rows, up_levels, up_scale, up_extra, up_pick)
    hidden = (jax.nn.silu(gate) * up).astype(jnp.bfloat16)
    mixed = lax.dynamic_slice_in_dim(mixed_all, lax.axis_index("tensor") * own_rows, own_rows, 0)
    down = lax.psum_scatter(
        project(hidden, down_levels, down_scale, down_extra, down_pick),
        "tensor",
        scatter_dimension=0,
        tiled=True,
    )
    return (mixed + down).astype(jnp.bfloat16)


def solution(mesh):
    placed = (
        P(("groups", "seq"), "tensor"),
        P(("groups", "seq", "tensor"), None),
        P("tensor", None),
        P(),
        P(),
        P(None, "tensor"),
        P("tensor"),
        P("tensor", None),
        P(None, "tensor"),
        P(None, "tensor"),
        P("tensor"),
        P("tensor", None),
        P(None, "tensor"),
        P("tensor", None),
        P(),
        P("tensor", None),
        P("tensor", None),
    )
    size = mesh.shape["tensor"]
    few = size <= 8 and size & (size - 1) == 0

    def local(*args):
        return direct(size, *args) if few else plain(*args)

    return jax.shard_map(
        local,
        mesh=mesh,
        in_specs=placed,
        out_specs=P(("groups", "seq", "tensor"), None),
        check_vma=False,
    )
```

```python
import jax
import jax.numpy as jnp
from jax import lax
from jax.experimental import pallas as pl
from jax.experimental.pallas import tpu as pltpu
from jax.sharding import PartitionSpec as P


VMEM = pl.BlockSpec(memory_space=pltpu.VMEM)
SMEM = pl.BlockSpec(memory_space=pltpu.SMEM)
HBM = pl.BlockSpec(memory_space=pltpu.HBM)
ANY = pl.BlockSpec(memory_space=pl.ANY)
EPS = 1e-05
LANES = 128
COVER_FLOPS = 10**12


def params(mib):
    return pltpu.CompilerParams(vmem_limit_bytes=mib * 1024 * 1024)


def whole_parts(size, want):
    for count in range(want, 0, -1):
        if size % (count * LANES) == 0:
            return count
    return 1


def proj_kernel(rows, parts, me_ref, heads_hbm, levels_hbm, scale_hbm, stream_hbm, gain_hbm, *refs):
    stream_ref, gain_ref = refs[:2]
    outs, (heads_ref, scale_ref, held, sems) = refs[2:-4], refs[-4:]
    pieces = len(outs)
    width = levels_hbm.shape[1] // parts

    def copy(i):
        return pltpu.make_async_copy(
            levels_hbm.at[:, pl.ds(i * width, width)], held.at[i], sems.at[i]
        )

    small = [
        pltpu.make_async_copy(source, target, sems.at[parts + n])
        for n, (source, target) in enumerate((
            (heads_hbm, heads_ref), (scale_hbm, scale_ref), (stream_hbm, stream_ref), (gain_hbm, gain_ref),
        ))
    ]
    small[0].start()
    small[1].start()
    for i in range(parts):
        copy(i).start()
    small[2].start()
    small[3].start()
    me = me_ref[0]
    tokens = pieces * rows
    line = lax.broadcasted_iota(jnp.int32, (tokens, tokens), 0)
    source = jnp.bitwise_xor(lax.div(line, rows), me) * rows + lax.rem(line, rows)
    moved = lax.broadcasted_iota(jnp.int32, (tokens, tokens), 1) == source
    moved = moved.astype(jnp.float32).astype(jnp.bfloat16)
    small[0].wait()
    lhs = jnp.dot(moved, heads_ref[...], preferred_element_type=jnp.float32).astype(jnp.bfloat16)
    small[1].wait()
    for i in range(parts):
        copy(i).wait()
        cols = slice(i * width, (i + 1) * width)
        partial = jnp.dot(lhs, held[i], preferred_element_type=jnp.float32)
        partial = partial * scale_ref[:, cols]
        for k in range(pieces):
            outs[k][:, cols] = partial[k * rows : (k + 1) * rows, :].astype(outs[k].dtype)
    small[2].wait()
    small[3].wait()


def project_out(me, heads, levels, scale, stream, gain, pieces):
    features, width = levels.shape
    rows = stream.shape[0]
    parts = whole_parts(width, 8)
    shapes = [jax.ShapeDtypeStruct(a.shape, a.dtype) for a in (stream, gain)]
    shapes += [jax.ShapeDtypeStruct((rows, width), jnp.float32)]
    shapes += [jax.ShapeDtypeStruct((rows, width), jnp.bfloat16)] * (pieces - 1)

    def body(*refs):
        proj_kernel(rows, parts, *refs)

    return pl.pallas_call(
        body,
        name="project_out",
        out_shape=shapes,
        in_specs=[SMEM] + [HBM] * 5,
        out_specs=[VMEM] * (pieces + 2),
        scratch_shapes=[
            pltpu.VMEM(heads.shape, heads.dtype),
            pltpu.VMEM(scale.shape, scale.dtype),
            pltpu.VMEM((parts, features, width // parts), jnp.bfloat16),
            pltpu.SemaphoreType.DMA((parts + 4,)),
        ],
        compiler_params=params(50),
    )(me, *[pltpu.with_memory_space_constraint(a, pltpu.HBM) for a in (heads, levels, scale, stream, gain)])


def norm_kernel(stream_ref, gain_ref, own_ref, *refs):
    others, (mixed_ref, normed_ref) = refs[:-2], refs[-2:]
    mixed = own_ref[...]
    for other in others:
        mixed = mixed + other[...].astype(jnp.float32)
    mixed = stream_ref[...].astype(jnp.float32) + mixed
    mixed_ref[...] = mixed
    mean_sq = jnp.mean(mixed * mixed, axis=-1, keepdims=True)
    normed_ref[...] = (mixed * lax.rsqrt(mean_sq + EPS) * gain_ref[...]).astype(jnp.bfloat16)


def mix_and_norm(stream, gain, own, others):
    return pl.pallas_call(
        norm_kernel,
        name="mix_and_norm",
        out_shape=[
            jax.ShapeDtypeStruct(own.shape, jnp.float32),
            jax.ShapeDtypeStruct(own.shape, jnp.bfloat16),
        ],
        in_specs=[VMEM] * (3 + len(others)),
        out_specs=[VMEM] * 2,
        cost_estimate=pl.CostEstimate(flops=COVER_FLOPS, transcendentals=0, bytes_accessed=0),
        compiler_params=params(2),
    )(stream, gain, own, *others)


def against(rows_in, extra):
    return lax.dot_general(
        rows_in, extra, (((1,), (1,)), ((), ())), preferred_element_type=jnp.float32
    )


def place(added, index_ref, first, width):
    count = added.shape[1]
    high = added.astype(jnp.bfloat16)
    low = (added - high.astype(jnp.float32)).astype(jnp.bfloat16)
    columns = lax.broadcasted_iota(jnp.int32, (count, width), 1) + first
    which = lax.broadcasted_iota(jnp.int32, (count, width), 0)
    target = jnp.full((count, width), -1, jnp.int32)
    for k in range(count):
        target = jnp.where(which == k, index_ref[0, k], target)
    chosen = (columns == target).astype(jnp.float32).astype(jnp.bfloat16)
    return jnp.dot(high, chosen, preferred_element_type=jnp.float32) + jnp.dot(
        low, chosen, preferred_element_type=jnp.float32
    )


def mlp_kernel(
    rows, depth, nup, ndown, parts,
    gate_scale_hbm, gate_index, gate_extra_hbm, up_scale_hbm, up_index, up_extra_hbm,
    down_scale_hbm, down_index, down_extra_hbm, gate_ref, up_hbm, down_hbm, *refs,
):
    (gate_scale, gate_extra, up_scale, up_extra, down_scale, down_extra,
     x_ref, gate_acc, up_acc, ring, held, ring_sems, held_sems, sems) = refs[-14:]
    refs = refs[:-14]
    pieces = len(refs) // 2
    ins, outs = refs[:pieces], refs[pieces:]
    width = down_hbm.shape[1] // parts
    steps = up_hbm.shape[0] // depth

    def feed(i):
        return pltpu.make_async_copy(
            up_hbm.at[pl.ds(i * depth, depth), :], ring.at[i % nup], ring_sems.at[i % nup]
        )

    def feed_down(i):
        return pltpu.make_async_copy(
            down_hbm.at[:, pl.ds(i * width, width)], held.at[i % ndown], held_sems.at[i % ndown]
        )

    small = [
        pltpu.make_async_copy(source, target, sems.at[n])
        for n, (source, target) in enumerate((
            (gate_scale_hbm, gate_scale), (gate_extra_hbm, gate_extra),
            (up_scale_hbm, up_scale), (up_extra_hbm, up_extra),
            (down_scale_hbm, down_scale), (down_extra_hbm, down_extra),
        ))
    ]
    for i in range(min(nup, steps)):
        feed(i).start()
    for copy in small:
        copy.start()
    stacked = jnp.concatenate([piece[...].astype(jnp.float32) for piece in ins], axis=0)
    x_ref[...] = stacked.astype(jnp.bfloat16)
    sent = 0
    for s in range(steps):
        span = slice(s * depth, (s + 1) * depth)
        lhs = x_ref[:, span]
        product = jnp.dot(lhs, gate_ref[span, :], preferred_element_type=jnp.float32)
        feed(s).wait()
        other = jnp.dot(lhs, ring[s % nup], preferred_element_type=jnp.float32)
        if s == 0:
            gate_acc[...] = product
            up_acc[...] = other
        else:
            gate_acc[...] += product
            up_acc[...] += other
        if s + nup < steps:
            feed(s + nup).start()
        elif sent < min(ndown, parts):
            feed_down(sent).start()
            sent += 1
    while sent < min(ndown, parts):
        feed_down(sent).start()
        sent += 1
    for copy in small:
        copy.wait()
    x = x_ref[...]
    shard = gate_acc.shape[1]
    gate = gate_acc[...] * gate_scale[...].reshape(1, shard) + place(against(x, gate_extra[...]), gate_index, 0, shard)
    up = up_acc[...] * up_scale[...].reshape(1, shard) + place(against(x, up_extra[...]), up_index, 0, shard)
    hidden = (gate / (1.0 + jnp.exp(-gate)) * up).astype(jnp.bfloat16)
    added = against(hidden, down_extra[...])
    for i in range(parts):
        feed_down(i).wait()
        cols = slice(i * width, (i + 1) * width)
        partial = jnp.dot(hidden, held[i % ndown], preferred_element_type=jnp.float32)
        if i + ndown < parts:
            feed_down(i + ndown).start()
        partial = partial * down_scale[:, cols] + place(added, down_index, i * width, width)
        for k in range(pieces):
            outs[k][:, cols] = partial[k * rows : (k + 1) * rows, :].astype(outs[k].dtype)


def mlp(normed, gate, up, down):
    gate_levels, gate_scale, gate_index, gate_extra = gate
    up_levels, up_scale, up_index, up_extra = up
    down_levels, down_scale, down_index, down_extra = down
    pieces, (rows, width) = len(normed), normed[0].shape
    shard = gate_levels.shape[1]
    tokens = pieces * rows
    parts = whole_parts(width, 8)
    depth = width // whole_parts(width, 16)
    nup, ndown = 4, 3
    shapes = [jax.ShapeDtypeStruct((rows, width), jnp.float32)]
    shapes += [jax.ShapeDtypeStruct((rows, width), jnp.bfloat16)] * (pieces - 1)

    def body(*refs):
        mlp_kernel(rows, depth, nup, ndown, parts, *refs)

    small = [gate_scale, gate_extra.T, up_scale, up_extra.T, down_scale[None], down_extra.T]
    return pl.pallas_call(
        body,
        name="mlp",
        out_shape=shapes,
        in_specs=[ANY, SMEM, ANY] * 3 + [VMEM, HBM, HBM] + [VMEM] * pieces,
        out_specs=[VMEM] * pieces,
        scratch_shapes=[pltpu.VMEM(a.shape, a.dtype) for a in small] + [
            pltpu.VMEM((tokens, width), jnp.bfloat16),
            pltpu.VMEM((tokens, shard), jnp.float32),
            pltpu.VMEM((tokens, shard), jnp.float32),
            pltpu.VMEM((nup, depth, shard), jnp.bfloat16),
            pltpu.VMEM((ndown, shard, width // parts), jnp.bfloat16),
            pltpu.SemaphoreType.DMA((nup,)),
            pltpu.SemaphoreType.DMA((ndown,)),
            pltpu.SemaphoreType.DMA((len(small),)),
        ],
        compiler_params=params(22),
    )(
        small[0], gate_index, small[1], small[2], up_index, small[3],
        small[4], down_index, small[5], gate_levels, up_levels, down_levels, *normed,
    )


def finish_kernel(mixed_ref, own_ref, *refs):
    others, out_ref = refs[:-1], refs[-1]
    down = own_ref[...]
    for other in others:
        down = down + other[...].astype(jnp.float32)
    out_ref[...] = (mixed_ref[...] + down).astype(jnp.bfloat16)


def finish(mixed, own, others):
    return pl.pallas_call(
        finish_kernel,
        name="finish",
        out_shape=jax.ShapeDtypeStruct(own.shape, jnp.bfloat16),
        in_specs=[VMEM] * (2 + len(others)),
        out_specs=VMEM,
        compiler_params=params(2),
    )(mixed, own, *others)


def exchange(arrays, size):
    return [
        lax.ppermute(array, "tensor", [(i, i ^ k) for i in range(size)])
        for k, array in enumerate(arrays, 1)
    ]


def direct(
    size, heads_out, stream_in, proj_levels, proj_scale, norm_gain,
    gate_levels, gate_scale, gate_index, gate_extra,
    up_levels, up_scale, up_index, up_extra,
    down_levels, down_scale, down_index, down_extra,
):
    me = lax.axis_index("tensor").astype(jnp.int32).reshape(1)
    stream, gain, own, *away = project_out(
        me, heads_out, proj_levels, proj_scale[None], stream_in, norm_gain[None], size
    )
    gate_levels = pltpu.with_memory_space_constraint(gate_levels, pltpu.VMEM)
    mixed, normed = mix_and_norm(stream, gain, own, exchange(away, size))
    gathered = [normed] + exchange([normed] * (size - 1), size)
    own, *away = mlp(
        gathered,
        (gate_levels, gate_scale, gate_index, gate_extra),
        (up_levels, up_scale, up_index, up_extra),
        (down_levels, down_scale, down_index, down_extra),
    )
    return finish(mixed, own, exchange(away, size))


def rms_norm(mixed, norm_gain):
    mean_sq = jnp.mean(mixed * mixed, axis=-1, keepdims=True)
    return (mixed * lax.rsqrt(mean_sq + EPS) * norm_gain).astype(jnp.bfloat16)


def picker(index_row, width):
    return (index_row[:, None] == jnp.arange(width, dtype=jnp.int32)[None, :]).astype(jnp.float32)


def project(rows_in, levels, scale, extra, chosen):
    base = jnp.dot(rows_in, levels, preferred_element_type=jnp.float32)
    added = jnp.dot(rows_in, extra, preferred_element_type=jnp.float32)
    return base * scale + jnp.dot(added, chosen, precision=lax.Precision.HIGHEST)


def plain(
    heads_out, stream_in, proj_levels, proj_scale, norm_gain,
    gate_levels, gate_scale, gate_index, gate_extra,
    up_levels, up_scale, up_index, up_extra,
    down_levels, down_scale, down_index, down_extra,
):
    own_rows = stream_in.shape[0]
    shard_width = gate_levels.shape[1]
    model_width = proj_levels.shape[1]
    gate_pick = picker(gate_index[0], shard_width)
    up_pick = picker(up_index[0], shard_width)
    down_pick = picker(down_index[0], model_width)
    total = lax.psum(
        jnp.dot(heads_out, proj_levels, preferred_element_type=jnp.float32) * proj_scale, "tensor"
    )
    stream_all = lax.all_gather(stream_in, "tensor", axis=0, tiled=True)
    mixed_all = stream_all.astype(jnp.float32) + total
    normed_rows = rms_norm(mixed_all, norm_gain)
    gate = project(normed_rows, gate_levels, gate_scale, gate_extra, gate_pick)
    up = project(normed_rows, up_levels, up_scale, up_extra, up_pick)
    hidden = (jax.nn.silu(gate) * up).astype(jnp.bfloat16)
    mixed = lax.dynamic_slice_in_dim(mixed_all, lax.axis_index("tensor") * own_rows, own_rows, 0)
    down = lax.psum_scatter(
        project(hidden, down_levels, down_scale, down_extra, down_pick),
        "tensor",
        scatter_dimension=0,
        tiled=True,
    )
    return (mixed + down).astype(jnp.bfloat16)


def solution(mesh):
    placed = (
        P(("groups", "seq"), "tensor"),
        P(("groups", "seq", "tensor"), None),
        P("tensor", None),
        P(),
        P(),
        P(None, "tensor"),
        P("tensor"),
        P("tensor", None),
        P(None, "tensor"),
        P(None, "tensor"),
        P("tensor"),
        P("tensor", None),
        P(None, "tensor"),
        P("tensor", None),
        P(),
        P("tensor", None),
        P("tensor", None),
    )
    size = mesh.shape["tensor"]
    few = size <= 8 and size & (size - 1) == 0

    def local(*args):
        return direct(size, *args) if few else plain(*args)

    return jax.shard_map(
        local,
        mesh=mesh,
        in_specs=placed,
        out_specs=P(("groups", "seq", "tensor"), None),
        check_vma=False,
    )
```

```python
import jax
import jax.numpy as jnp
from jax import lax
from jax.experimental import pallas as pl
from jax.experimental.pallas import tpu as pltpu
from jax.sharding import PartitionSpec as P


VMEM = pl.BlockSpec(memory_space=pltpu.VMEM)
SMEM = pl.BlockSpec(memory_space=pltpu.SMEM)
HBM = pl.BlockSpec(memory_space=pltpu.HBM)
ANY = pl.BlockSpec(memory_space=pl.ANY)
EPS = 1e-05
LANES = 128
COVER_FLOPS = 10**12
MLP_MIB = 14
DEPTH = 512
PART = 256
SLOTS = 6
LEAD = 1


def params(mib):
    return pltpu.CompilerParams(vmem_limit_bytes=mib * 1024 * 1024)


def whole_parts(size, want):
    for count in range(want, 0, -1):
        if size % (count * LANES) == 0:
            return count
    return 1


def chunk_of(size, want):
    return size // whole_parts(size, want)


def piece_shapes(rows, width, pieces):
    kinds = (jnp.float32, jnp.bfloat16)
    return [jax.ShapeDtypeStruct((rows, width), kinds[k % 2]) for k in range(pieces)]


def proj_kernel(rows, parts, me_ref, heads_hbm, levels_hbm, scale_hbm, stream_hbm, gain_hbm, *refs):
    stream_ref, gain_ref = refs[:2]
    outs, (heads_ref, scale_ref, held, sems) = refs[2:-4], refs[-4:]
    pieces = len(outs)
    width = levels_hbm.shape[1] // parts

    def copy(i):
        return pltpu.make_async_copy(
            levels_hbm.at[:, pl.ds(i * width, width)], held.at[i], sems.at[i]
        )

    small = [
        pltpu.make_async_copy(source, target, sems.at[parts + n])
        for n, (source, target) in enumerate((
            (heads_hbm, heads_ref), (scale_hbm, scale_ref), (stream_hbm, stream_ref), (gain_hbm, gain_ref),
        ))
    ]
    small[0].start()
    small[1].start()
    for i in range(parts):
        copy(i).start()
    small[2].start()
    small[3].start()
    me = me_ref[0]
    tokens = pieces * rows
    line = lax.broadcasted_iota(jnp.int32, (tokens, tokens), 0)
    source = jnp.bitwise_xor(lax.div(line, rows), me) * rows + lax.rem(line, rows)
    moved = lax.broadcasted_iota(jnp.int32, (tokens, tokens), 1) == source
    moved = moved.astype(jnp.float32).astype(jnp.bfloat16)
    small[0].wait()
    lhs = jnp.dot(moved, heads_ref[...], preferred_element_type=jnp.float32).astype(jnp.bfloat16)
    small[1].wait()
    for i in range(parts):
        copy(i).wait()
        cols = slice(i * width, (i + 1) * width)
        partial = jnp.dot(lhs, held[i], preferred_element_type=jnp.float32)
        partial = partial * scale_ref[:, cols]
        for k in range(pieces):
            outs[k][:, cols] = partial[k * rows : (k + 1) * rows, :].astype(outs[k].dtype)
    small[2].wait()
    small[3].wait()


def project_out(me, heads, levels, scale, stream, gain, pieces):
    features, width = levels.shape
    rows = stream.shape[0]
    parts = whole_parts(width, 8)
    shapes = [jax.ShapeDtypeStruct(a.shape, a.dtype) for a in (stream, gain)]
    shapes += piece_shapes(rows, width, pieces)

    def body(*refs):
        proj_kernel(rows, parts, *refs)

    return pl.pallas_call(
        body,
        name="project_out",
        out_shape=shapes,
        in_specs=[SMEM] + [HBM] * 5,
        out_specs=[VMEM] * (pieces + 2),
        scratch_shapes=[
            pltpu.VMEM(heads.shape, heads.dtype),
            pltpu.VMEM(scale.shape, scale.dtype),
            pltpu.VMEM((parts, features, width // parts), jnp.bfloat16),
            pltpu.SemaphoreType.DMA((parts + 4,)),
        ],
        compiler_params=params(50),
    )(me, *[pltpu.with_memory_space_constraint(a, pltpu.HBM) for a in (heads, levels, scale, stream, gain)])


def norm_kernel(after_ref, stream_ref, gain_ref, own_ref, *refs):
    del after_ref
    others, (mixed_ref, normed_ref) = refs[:-2], refs[-2:]
    mixed = own_ref[...]
    for other in others:
        mixed = mixed + other[...].astype(jnp.float32)
    mixed = stream_ref[...].astype(jnp.float32) + mixed
    mixed_ref[...] = mixed
    mean_sq = jnp.mean(mixed * mixed, axis=-1, keepdims=True)
    normed_ref[...] = (mixed * lax.rsqrt(mean_sq + EPS) * gain_ref[...]).astype(jnp.bfloat16)


def mix_and_norm(after, stream, gain, own, others):
    return pl.pallas_call(
        norm_kernel,
        name="mix_and_norm",
        out_shape=[
            jax.ShapeDtypeStruct(own.shape, jnp.float32),
            jax.ShapeDtypeStruct(own.shape, jnp.bfloat16),
        ],
        in_specs=[ANY] + [VMEM] * (3 + len(others)),
        out_specs=[VMEM] * 2,
        cost_estimate=pl.CostEstimate(flops=COVER_FLOPS, transcendentals=0, bytes_accessed=0),
        compiler_params=params(2),
    )(after, stream, gain, own, *others)


def preload(levels, columns):
    depth = levels.shape[0]
    step = columns // whole_parts(columns, 8)

    def body(levels_hbm, held, sems):
        copies = [
            pltpu.make_async_copy(
                levels_hbm.at[:, pl.ds(first, step)], held.at[:, pl.ds(first, step)], sems.at[first // step]
            )
            for first in range(0, columns, step)
        ]
        for copy in copies:
            copy.start()
        for copy in copies:
            copy.wait()

    held = pl.pallas_call(
        body,
        name="preload",
        out_shape=jax.ShapeDtypeStruct((depth, columns), levels.dtype),
        in_specs=[HBM],
        out_specs=VMEM,
        scratch_shapes=[pltpu.SemaphoreType.DMA((columns // step,))],
        cost_estimate=pl.CostEstimate(flops=10**10, transcendentals=0, bytes_accessed=0),
        compiler_params=params(1),
    )(pltpu.with_memory_space_constraint(levels, pltpu.HBM))
    return pltpu.with_memory_space_constraint(held, pltpu.VMEM)


def early_columns(levels):
    shard, width = levels.shape
    return width - (3 * width // 4) // shard * shard


def against(rows_in, extra):
    return lax.dot_general(
        rows_in, extra, (((1,), (1,)), ((), ())), preferred_element_type=jnp.float32
    )


def halves(added):
    high = added.astype(jnp.bfloat16).astype(jnp.float32)
    return jnp.concatenate([high, added - high], axis=1).astype(jnp.bfloat16)


def place(split, index_ref, first, width):
    count = split.shape[1]
    columns = lax.broadcasted_iota(jnp.int32, (count, width), 1) + first
    which = lax.broadcasted_iota(jnp.int32, (count, 1), 0)
    target = jnp.zeros((count, 1), jnp.int32)
    for k in range(count):
        target = jnp.where(which == k, index_ref[0, k % (count // 2)], target)
    chosen = (columns == target).astype(jnp.float32).astype(jnp.bfloat16)
    return jnp.dot(split, chosen, preferred_element_type=jnp.float32)


def mlp_kernel(
    rows, depth, part, lead,
    gate_scale, gate_index, gate_extra, up_scale, up_index, up_extra,
    down_scale, down_index, down_extra, gate_ref, first_ref, up_hbm, down_hbm, *refs,
):
    (x_ref, hidden_ref, gate_acc, up_acc, ring, ring_sems) = refs[-6:]
    refs = refs[:-6]
    pieces = len(refs) // 2
    ins, outs = refs[:pieces], refs[pieces:]
    slots = ring.shape[0]
    ready = first_ref.shape[1]
    shard = gate_acc.shape[1]
    steps = up_hbm.shape[0] // depth
    groups = (down_hbm.shape[1] - ready) // shard

    blocks = [(up_hbm.at[pl.ds(i * depth, depth), :], depth) for i in range(steps)]
    for c in range(groups):
        for first in range(0, shard, depth):
            count = min(depth, shard - first)
            source = down_hbm.at[pl.ds(first, count), pl.ds(ready + c * shard, shard)]
            blocks.append((source, count))

    def copies(i):
        source, count = blocks[i]
        return [
            pltpu.make_async_copy(
                source.at[pl.ds(n, part), :],
                ring.at[i % slots, pl.ds(n, part), :],
                ring_sems.at[i % slots, n // part],
            )
            for n in range(0, count, part)
        ]

    def start(i):
        if i < len(blocks):
            for copy in copies(i):
                copy.start()

    def arrive(i):
        for copy in copies(i):
            copy.wait()
        return ring[i % slots, : blocks[i][1], :]

    for i in range(slots):
        start(i)
    stacked = jnp.concatenate([piece[...].astype(jnp.float32) for piece in ins], axis=0)
    x_ref[...] = stacked.astype(jnp.bfloat16)

    def add(acc, s, weights):
        product = jnp.dot(
            x_ref[:, s * depth : (s + 1) * depth], weights, preferred_element_type=jnp.float32
        )
        acc[...] = product if s == 0 else acc[...] + product

    for s in range(lead + steps):
        if s < steps:
            add(gate_acc, s, gate_ref[s * depth : (s + 1) * depth, :])
        if s >= lead:
            i = s - lead
            add(up_acc, i, arrive(i))
            start(i + slots)
    x = x_ref[...]
    gate_more = place(halves(against(x, gate_extra[...])), gate_index, 0, shard)
    up_more = place(halves(against(x, up_extra[...])), up_index, 0, shard)
    gate = gate_acc[...] * gate_scale[...].reshape(1, shard) + gate_more
    up = up_acc[...] * up_scale[...].reshape(1, shard) + up_more
    hidden_ref[...] = (gate / (1.0 + jnp.exp(-gate)) * up).astype(jnp.bfloat16)
    hidden = hidden_ref[...]
    split = halves(against(hidden, down_extra[...]))

    def leave(total, first, count):
        cols = slice(first, first + count)
        total = total * down_scale[:, cols] + place(split, down_index, first, count)
        for k in range(pieces):
            outs[k][:, cols] = total[k * rows : (k + 1) * rows, :].astype(outs[k].dtype)

    span = chunk_of(ready, 2)
    for first in range(0, ready, span):
        leave(
            jnp.dot(hidden, first_ref[:, first : first + span], preferred_element_type=jnp.float32),
            first, span,
        )
    i = steps
    for c in range(groups):
        total = None
        for first in range(0, shard, depth):
            count = blocks[i][1]
            product = jnp.dot(
                hidden_ref[:, first : first + count], arrive(i), preferred_element_type=jnp.float32
            )
            total = product if total is None else total + product
            start(i + slots)
            i += 1
        leave(total, ready + c * shard, shard)


def mlp(normed, gate, up, down):
    gate_levels, gate_scale, gate_index, gate_extra = gate
    up_levels, up_scale, up_index, up_extra = up
    down_first, down_levels, down_scale, down_index, down_extra = down
    pieces, (rows, width) = len(normed), normed[0].shape
    shard = gate_levels.shape[1]
    tokens = pieces * rows
    shapes = piece_shapes(rows, width, pieces)

    def body(*refs):
        mlp_kernel(rows, DEPTH, PART, LEAD, *refs)

    small = [gate_scale, gate_extra.T, up_scale, up_extra.T, down_scale[None], down_extra.T]
    return pl.pallas_call(
        body,
        name="mlp",
        out_shape=shapes,
        in_specs=[VMEM, SMEM, VMEM] * 3 + [VMEM, VMEM, HBM, HBM] + [VMEM] * pieces,
        out_specs=[VMEM] * pieces,
        scratch_shapes=[
            pltpu.VMEM((tokens, width), jnp.bfloat16),
            pltpu.VMEM((tokens, shard), jnp.bfloat16),
            pltpu.VMEM((tokens, shard), jnp.float32),
            pltpu.VMEM((tokens, shard), jnp.float32),
            pltpu.VMEM((SLOTS, DEPTH, shard), jnp.bfloat16),
            pltpu.SemaphoreType.DMA((SLOTS, DEPTH // PART)),
        ],
        compiler_params=params(MLP_MIB),
    )(
        small[0], gate_index, small[1], small[2], up_index, small[3],
        small[4], down_index, small[5], gate_levels, down_first, up_levels, down_levels, *normed,
    )


def finish_kernel(mixed_ref, own_ref, *refs):
    others, out_ref = refs[:-1], refs[-1]
    down = own_ref[...]
    for other in others:
        down = down + other[...].astype(jnp.float32)
    out_ref[...] = (mixed_ref[...] + down).astype(jnp.bfloat16)


def finish(mixed, own, others):
    return pl.pallas_call(
        finish_kernel,
        name="finish",
        out_shape=jax.ShapeDtypeStruct(own.shape, jnp.bfloat16),
        in_specs=[VMEM] * (2 + len(others)),
        out_specs=VMEM,
        compiler_params=params(2),
    )(mixed, own, *others)


def moved(array, k, size):
    return lax.ppermute(array, "tensor", [(i, i ^ k) for i in range(size)])


def merge_kernel(*refs):
    count = len(refs) // 3
    for kept, passed, out in zip(refs[:count], refs[count : 2 * count], refs[2 * count :]):
        out[...] = (kept[...] + passed[...].astype(jnp.float32)).astype(out.dtype)


def scatter(pieces, size):
    passed = {k ^ 1: moved(pieces[k], 1, size) for k in range(size - 1, 0, -2)}
    far = list(range(size - 2, 0, -2))
    kept = [pieces[k] for k in far]
    merged = pl.pallas_call(
        merge_kernel,
        name="merge",
        out_shape=[jax.ShapeDtypeStruct(a.shape, jnp.bfloat16) for a in kept],
        in_specs=[VMEM] * (2 * len(kept)),
        out_specs=[VMEM] * len(kept),
        compiler_params=params(2),
    )(*kept, *[passed[k] for k in far])
    return pieces[0], [passed[0]] + [moved(a, k, size) for a, k in zip(merged, far)]


def gather(piece, size):
    pieces = [piece] + [moved(piece, k, size) for k in range(2, size, 2)]
    passed = [moved(near, 1, size) for near in pieces]
    return [one for pair in zip(pieces, passed) for one in pair]


def direct(
    size, heads_out, stream_in, proj_levels, proj_scale, norm_gain,
    gate_levels, gate_scale, gate_index, gate_extra,
    up_levels, up_scale, up_index, up_extra,
    down_levels, down_scale, down_index, down_extra,
):
    me = lax.axis_index("tensor").astype(jnp.int32).reshape(1)
    stream, gain, *terms = project_out(
        me, heads_out, proj_levels, proj_scale[None], stream_in, norm_gain[None], size
    )
    down_first = preload(down_levels, early_columns(down_levels))
    gate_levels = pltpu.with_memory_space_constraint(gate_levels, pltpu.VMEM)
    mixed, normed = mix_and_norm(down_first, stream, gain, *scatter(terms, size))
    gathered = gather(normed, size)
    terms = mlp(
        gathered,
        (gate_levels, gate_scale, gate_index, gate_extra),
        (up_levels, up_scale, up_index, up_extra),
        (down_first, down_levels, down_scale, down_index, down_extra),
    )
    return finish(mixed, *scatter(terms, size))


def rms_norm(mixed, norm_gain):
    mean_sq = jnp.mean(mixed * mixed, axis=-1, keepdims=True)
    return (mixed * lax.rsqrt(mean_sq + EPS) * norm_gain).astype(jnp.bfloat16)


def picker(index_row, width):
    return (index_row[:, None] == jnp.arange(width, dtype=jnp.int32)[None, :]).astype(jnp.float32)


def project(rows_in, levels, scale, extra, chosen):
    base = jnp.dot(rows_in, levels, preferred_element_type=jnp.float32)
    added = jnp.dot(rows_in, extra, preferred_element_type=jnp.float32)
    return base * scale + jnp.dot(added, chosen, precision=lax.Precision.HIGHEST)


def plain(
    heads_out, stream_in, proj_levels, proj_scale, norm_gain,
    gate_levels, gate_scale, gate_index, gate_extra,
    up_levels, up_scale, up_index, up_extra,
    down_levels, down_scale, down_index, down_extra,
):
    own_rows = stream_in.shape[0]
    shard_width = gate_levels.shape[1]
    model_width = proj_levels.shape[1]
    gate_pick = picker(gate_index[0], shard_width)
    up_pick = picker(up_index[0], shard_width)
    down_pick = picker(down_index[0], model_width)
    total = lax.psum(
        jnp.dot(heads_out, proj_levels, preferred_element_type=jnp.float32) * proj_scale, "tensor"
    )
    stream_all = lax.all_gather(stream_in, "tensor", axis=0, tiled=True)
    mixed_all = stream_all.astype(jnp.float32) + total
    normed_rows = rms_norm(mixed_all, norm_gain)
    gate = project(normed_rows, gate_levels, gate_scale, gate_extra, gate_pick)
    up = project(normed_rows, up_levels, up_scale, up_extra, up_pick)
    hidden = (jax.nn.silu(gate) * up).astype(jnp.bfloat16)
    mixed = lax.dynamic_slice_in_dim(mixed_all, lax.axis_index("tensor") * own_rows, own_rows, 0)
    down = lax.psum_scatter(
        project(hidden, down_levels, down_scale, down_extra, down_pick),
        "tensor",
        scatter_dimension=0,
        tiled=True,
    )
    return (mixed + down).astype(jnp.bfloat16)


def solution(mesh):
    placed = (
        P(("groups", "seq"), "tensor"),
        P(("groups", "seq", "tensor"), None),
        P("tensor", None),
        P(),
        P(),
        P(None, "tensor"),
        P("tensor"),
        P("tensor", None),
        P(None, "tensor"),
        P(None, "tensor"),
        P("tensor"),
        P("tensor", None),
        P(None, "tensor"),
        P("tensor", None),
        P(),
        P("tensor", None),
        P("tensor", None),
    )
    size = mesh.shape["tensor"]
    few = 4 <= size <= 8 and size & (size - 1) == 0

    def local(*args):
        return direct(size, *args) if few else plain(*args)

    return jax.shard_map(
        local,
        mesh=mesh,
        in_specs=placed,
        out_specs=P(("groups", "seq", "tensor"), None),
        check_vma=False,
    )
```

```python
import jax
import jax.numpy as jnp
from jax import lax
from jax.experimental import pallas as pl
from jax.experimental.pallas import tpu as pltpu
from jax.sharding import PartitionSpec as P


VMEM = pl.BlockSpec(memory_space=pltpu.VMEM)
SMEM = pl.BlockSpec(memory_space=pltpu.SMEM)
HBM = pl.BlockSpec(memory_space=pltpu.HBM)
ANY = pl.BlockSpec(memory_space=pl.ANY)
EPS = 1e-05
LANES = 128
COVER_FLOPS = 10**12
MLP_MIB = 14
DEPTH = 512
PART = 256
SLOTS = 6
LEAD = 1


def params(mib):
    return pltpu.CompilerParams(vmem_limit_bytes=mib * 1024 * 1024)


def whole_parts(size, want):
    for count in range(want, 0, -1):
        if size % (count * LANES) == 0:
            return count
    return 1


def chunk_of(size, want):
    return size // whole_parts(size, want)


def piece_shapes(rows, width, pieces):
    kinds = (jnp.float32, jnp.bfloat16)
    return [jax.ShapeDtypeStruct((rows, width), kinds[k % 2]) for k in range(pieces)]


def proj_kernel(rows, parts, me_ref, heads_hbm, levels_hbm, scale_hbm, stream_hbm, gain_hbm, *refs):
    stream_ref, gain_ref = refs[:2]
    outs, (heads_ref, scale_ref, held, sems) = refs[2:-4], refs[-4:]
    pieces = len(outs)
    width = levels_hbm.shape[1] // parts

    def copy(i):
        return pltpu.make_async_copy(
            levels_hbm.at[:, pl.ds(i * width, width)], held.at[i], sems.at[i]
        )

    small = [
        pltpu.make_async_copy(source, target, sems.at[parts + n])
        for n, (source, target) in enumerate((
            (heads_hbm, heads_ref), (scale_hbm, scale_ref), (stream_hbm, stream_ref), (gain_hbm, gain_ref),
        ))
    ]
    small[0].start()
    small[1].start()
    for i in range(parts):
        copy(i).start()
    small[2].start()
    small[3].start()
    me = me_ref[0]
    tokens = pieces * rows
    line = lax.broadcasted_iota(jnp.int32, (tokens, tokens), 0)
    source = jnp.bitwise_xor(lax.div(line, rows), me) * rows + lax.rem(line, rows)
    moved = lax.broadcasted_iota(jnp.int32, (tokens, tokens), 1) == source
    moved = moved.astype(jnp.float32).astype(jnp.bfloat16)
    small[0].wait()
    lhs = jnp.dot(moved, heads_ref[...], preferred_element_type=jnp.float32).astype(jnp.bfloat16)
    small[1].wait()
    for i in range(parts):
        copy(i).wait()
        cols = slice(i * width, (i + 1) * width)
        partial = jnp.dot(lhs, held[i], preferred_element_type=jnp.float32)
        partial = partial * scale_ref[:, cols]
        for k in range(pieces):
            outs[k][:, cols] = partial[k * rows : (k + 1) * rows, :].astype(outs[k].dtype)
    small[2].wait()
    small[3].wait()


def project_out(me, heads, levels, scale, stream, gain, pieces):
    features, width = levels.shape
    rows = stream.shape[0]
    parts = whole_parts(width, 8)
    shapes = [jax.ShapeDtypeStruct(a.shape, a.dtype) for a in (stream, gain)]
    shapes += piece_shapes(rows, width, pieces)

    def body(*refs):
        proj_kernel(rows, parts, *refs)

    return pl.pallas_call(
        body,
        name="project_out",
        out_shape=shapes,
        in_specs=[SMEM] + [HBM] * 5,
        out_specs=[VMEM] * (pieces + 2),
        scratch_shapes=[
            pltpu.VMEM(heads.shape, heads.dtype),
            pltpu.VMEM(scale.shape, scale.dtype),
            pltpu.VMEM((parts, features, width // parts), jnp.bfloat16),
            pltpu.SemaphoreType.DMA((parts + 4,)),
        ],
        compiler_params=params(50),
    )(me, *[pltpu.with_memory_space_constraint(a, pltpu.HBM) for a in (heads, levels, scale, stream, gain)])


def norm_kernel(after_ref, stream_ref, gain_ref, own_ref, *refs):
    del after_ref
    others, (mixed_ref, normed_ref) = refs[:-2], refs[-2:]
    mixed = own_ref[...]
    for other in others:
        mixed = mixed + other[...].astype(jnp.float32)
    mixed = stream_ref[...].astype(jnp.float32) + mixed
    mixed_ref[...] = mixed
    mean_sq = jnp.mean(mixed * mixed, axis=-1, keepdims=True)
    normed_ref[...] = (mixed * lax.rsqrt(mean_sq + EPS) * gain_ref[...]).astype(jnp.bfloat16)


def mix_and_norm(after, stream, gain, own, others):
    return pl.pallas_call(
        norm_kernel,
        name="mix_and_norm",
        out_shape=[
            jax.ShapeDtypeStruct(own.shape, jnp.float32),
            jax.ShapeDtypeStruct(own.shape, jnp.bfloat16),
        ],
        in_specs=[ANY] + [VMEM] * (3 + len(others)),
        out_specs=[VMEM] * 2,
        cost_estimate=pl.CostEstimate(flops=COVER_FLOPS, transcendentals=0, bytes_accessed=0),
        compiler_params=params(2),
    )(after, stream, gain, own, *others)


def preload(levels, columns):
    depth = levels.shape[0]
    step = columns // whole_parts(columns, 8)

    def body(levels_hbm, held, sems):
        copies = [
            pltpu.make_async_copy(
                levels_hbm.at[:, pl.ds(first, step)], held.at[:, pl.ds(first, step)], sems.at[first // step]
            )
            for first in range(0, columns, step)
        ]
        for copy in copies:
            copy.start()
        for copy in copies:
            copy.wait()

    held = pl.pallas_call(
        body,
        name="preload",
        out_shape=jax.ShapeDtypeStruct((depth, columns), levels.dtype),
        in_specs=[HBM],
        out_specs=VMEM,
        scratch_shapes=[pltpu.SemaphoreType.DMA((columns // step,))],
        cost_estimate=pl.CostEstimate(flops=10**10, transcendentals=0, bytes_accessed=0),
        compiler_params=params(1),
    )(pltpu.with_memory_space_constraint(levels, pltpu.HBM))
    return pltpu.with_memory_space_constraint(held, pltpu.VMEM)


def early_columns(levels):
    shard, width = levels.shape
    return width - (3 * width // 4) // shard * shard


def against(rows_in, extra):
    return lax.dot_general(
        rows_in, extra, (((1,), (1,)), ((), ())), preferred_element_type=jnp.float32
    )


def halves(added):
    high = added.astype(jnp.bfloat16).astype(jnp.float32)
    return jnp.concatenate([high, added - high], axis=1).astype(jnp.bfloat16)


def place(split, index_ref, first, width):
    count = split.shape[1]
    columns = lax.broadcasted_iota(jnp.int32, (count, width), 1) + first
    which = lax.broadcasted_iota(jnp.int32, (count, 1), 0)
    target = jnp.zeros((count, 1), jnp.int32)
    for k in range(count):
        target = jnp.where(which == k, index_ref[0, k % (count // 2)], target)
    chosen = (columns == target).astype(jnp.float32).astype(jnp.bfloat16)
    return jnp.dot(split, chosen, preferred_element_type=jnp.float32)


def mlp_kernel(
    rows, depth, part, lead,
    gate_scale, gate_index, gate_extra, up_scale, up_index, up_extra,
    down_scale, down_index, down_extra, gate_ref, first_ref, up_hbm, down_hbm, *refs,
):
    (x_ref, hidden_ref, gate_acc, up_acc, ring, ring_sems) = refs[-6:]
    refs = refs[:-6]
    pieces = len(refs) // 2
    ins, outs = refs[:pieces], refs[pieces:]
    slots = ring.shape[0]
    ready = first_ref.shape[1]
    shard = gate_acc.shape[1]
    steps = up_hbm.shape[0] // depth
    groups = (down_hbm.shape[1] - ready) // shard

    blocks = [(up_hbm.at[pl.ds(i * depth, depth), :], depth) for i in range(steps)]
    for c in range(groups):
        for first in range(0, shard, depth):
            count = min(depth, shard - first)
            source = down_hbm.at[pl.ds(first, count), pl.ds(ready + c * shard, shard)]
            blocks.append((source, count))

    def copies(i):
        source, count = blocks[i]
        return [
            pltpu.make_async_copy(
                source.at[pl.ds(n, part), :],
                ring.at[i % slots, pl.ds(n, part), :],
                ring_sems.at[i % slots, n // part],
            )
            for n in range(0, count, part)
        ]

    def start(i):
        if i < len(blocks):
            for copy in copies(i):
                copy.start()

    def arrive(i):
        for copy in copies(i):
            copy.wait()
        return ring[i % slots, : blocks[i][1], :]

    for i in range(slots):
        start(i)
    stacked = jnp.concatenate([piece[...].astype(jnp.float32) for piece in ins], axis=0)
    x_ref[...] = stacked.astype(jnp.bfloat16)

    def add(acc, s, weights):
        product = jnp.dot(
            x_ref[:, s * depth : (s + 1) * depth], weights, preferred_element_type=jnp.float32
        )
        acc[...] = product if s == 0 else acc[...] + product

    for s in range(lead + steps):
        if s < steps:
            add(gate_acc, s, gate_ref[s * depth : (s + 1) * depth, :])
        if s >= lead:
            i = s - lead
            add(up_acc, i, arrive(i))
            start(i + slots)
    x = x_ref[...]
    gate_more = place(halves(against(x, gate_extra[...])), gate_index, 0, shard)
    up_more = place(halves(against(x, up_extra[...])), up_index, 0, shard)
    gate = gate_acc[...] * gate_scale[...].reshape(1, shard) + gate_more
    up = up_acc[...] * up_scale[...].reshape(1, shard) + up_more
    hidden_ref[...] = (gate / (1.0 + jnp.exp(-gate)) * up).astype(jnp.bfloat16)
    hidden = hidden_ref[...]
    split = halves(against(hidden, down_extra[...]))

    def leave(total, first, count):
        cols = slice(first, first + count)
        total = total * down_scale[:, cols] + place(split, down_index, first, count)
        for k in range(pieces):
            outs[k][:, cols] = total[k * rows : (k + 1) * rows, :].astype(outs[k].dtype)

    span = chunk_of(ready, 2)
    for first in range(0, ready, span):
        leave(
            jnp.dot(hidden, first_ref[:, first : first + span], preferred_element_type=jnp.float32),
            first, span,
        )
    i = steps
    for c in range(groups):
        total = None
        for first in range(0, shard, depth):
            count = blocks[i][1]
            product = jnp.dot(
                hidden_ref[:, first : first + count], arrive(i), preferred_element_type=jnp.float32
            )
            total = product if total is None else total + product
            start(i + slots)
            i += 1
        leave(total, ready + c * shard, shard)


def mlp(normed, gate, up, down):
    gate_levels, gate_scale, gate_index, gate_extra = gate
    up_levels, up_scale, up_index, up_extra = up
    down_first, down_levels, down_scale, down_index, down_extra = down
    pieces, (rows, width) = len(normed), normed[0].shape
    shard = gate_levels.shape[1]
    tokens = pieces * rows
    shapes = piece_shapes(rows, width, pieces)

    def body(*refs):
        mlp_kernel(rows, DEPTH, PART, LEAD, *refs)

    small = [gate_scale, gate_extra.T, up_scale, up_extra.T, down_scale[None], down_extra.T]
    return pl.pallas_call(
        body,
        name="mlp",
        out_shape=shapes,
        in_specs=[VMEM, SMEM, VMEM] * 3 + [VMEM, VMEM, HBM, HBM] + [VMEM] * pieces,
        out_specs=[VMEM] * pieces,
        scratch_shapes=[
            pltpu.VMEM((tokens, width), jnp.bfloat16),
            pltpu.VMEM((tokens, shard), jnp.bfloat16),
            pltpu.VMEM((tokens, shard), jnp.float32),
            pltpu.VMEM((tokens, shard), jnp.float32),
            pltpu.VMEM((SLOTS, DEPTH, shard), jnp.bfloat16),
            pltpu.SemaphoreType.DMA((SLOTS, DEPTH // PART)),
        ],
        compiler_params=params(MLP_MIB),
    )(
        small[0], gate_index, small[1], small[2], up_index, small[3],
        small[4], down_index, small[5], gate_levels, down_first, up_levels, down_levels, *normed,
    )


def finish_kernel(mixed_ref, own_ref, *refs):
    others, out_ref = refs[:-1], refs[-1]
    down = own_ref[...]
    for other in others:
        down = down + other[...].astype(jnp.float32)
    out_ref[...] = (mixed_ref[...] + down).astype(jnp.bfloat16)


def finish(mixed, own, others):
    return pl.pallas_call(
        finish_kernel,
        name="finish",
        out_shape=jax.ShapeDtypeStruct(own.shape, jnp.bfloat16),
        in_specs=[VMEM] * (2 + len(others)),
        out_specs=VMEM,
        compiler_params=params(2),
    )(mixed, own, *others)


def moved(array, k, size):
    return lax.ppermute(array, "tensor", [(i, i ^ k) for i in range(size)])


def merge_kernel(kept_ref, passed_ref, out_ref):
    out_ref[...] = (kept_ref[...] + passed_ref[...].astype(jnp.float32)).astype(out_ref.dtype)


def merge(kept, passed):
    return pl.pallas_call(
        merge_kernel,
        name="merge",
        out_shape=jax.ShapeDtypeStruct(kept.shape, passed.dtype),
        in_specs=[VMEM] * 2,
        out_specs=VMEM,
        compiler_params=params(1),
    )(kept, passed)


def scatter(pieces, size):
    passed = {k ^ 1: moved(pieces[k], 1, size) for k in range(size - 1, 0, -2)}
    far = range(size - 2, 0, -2)
    return pieces[0], [passed[0]] + [moved(merge(pieces[k], passed[k]), k, size) for k in far]


def gather(piece, size):
    pieces = [piece] + [moved(piece, k, size) for k in range(2, size, 2)]
    passed = [moved(near, 1, size) for near in pieces]
    return [one for pair in zip(pieces, passed) for one in pair]


def direct(
    size, heads_out, stream_in, proj_levels, proj_scale, norm_gain,
    gate_levels, gate_scale, gate_index, gate_extra,
    up_levels, up_scale, up_index, up_extra,
    down_levels, down_scale, down_index, down_extra,
):
    me = lax.axis_index("tensor").astype(jnp.int32).reshape(1)
    stream, gain, *terms = project_out(
        me, heads_out, proj_levels, proj_scale[None], stream_in, norm_gain[None], size
    )
    down_first = preload(down_levels, early_columns(down_levels))
    gate_levels = pltpu.with_memory_space_constraint(gate_levels, pltpu.VMEM)
    mixed, normed = mix_and_norm(down_first, stream, gain, *scatter(terms, size))
    gathered = gather(normed, size)
    terms = mlp(
        gathered,
        (gate_levels, gate_scale, gate_index, gate_extra),
        (up_levels, up_scale, up_index, up_extra),
        (down_first, down_levels, down_scale, down_index, down_extra),
    )
    return finish(mixed, *scatter(terms, size))


def rms_norm(mixed, norm_gain):
    mean_sq = jnp.mean(mixed * mixed, axis=-1, keepdims=True)
    return (mixed * lax.rsqrt(mean_sq + EPS) * norm_gain).astype(jnp.bfloat16)


def picker(index_row, width):
    return (index_row[:, None] == jnp.arange(width, dtype=jnp.int32)[None, :]).astype(jnp.float32)


def project(rows_in, levels, scale, extra, chosen):
    base = jnp.dot(rows_in, levels, preferred_element_type=jnp.float32)
    added = jnp.dot(rows_in, extra, preferred_element_type=jnp.float32)
    return base * scale + jnp.dot(added, chosen, precision=lax.Precision.HIGHEST)


def plain(
    heads_out, stream_in, proj_levels, proj_scale, norm_gain,
    gate_levels, gate_scale, gate_index, gate_extra,
    up_levels, up_scale, up_index, up_extra,
    down_levels, down_scale, down_index, down_extra,
):
    own_rows = stream_in.shape[0]
    shard_width = gate_levels.shape[1]
    model_width = proj_levels.shape[1]
    gate_pick = picker(gate_index[0], shard_width)
    up_pick = picker(up_index[0], shard_width)
    down_pick = picker(down_index[0], model_width)
    total = lax.psum(
        jnp.dot(heads_out, proj_levels, preferred_element_type=jnp.float32) * proj_scale, "tensor"
    )
    stream_all = lax.all_gather(stream_in, "tensor", axis=0, tiled=True)
    mixed_all = stream_all.astype(jnp.float32) + total
    normed_rows = rms_norm(mixed_all, norm_gain)
    gate = project(normed_rows, gate_levels, gate_scale, gate_extra, gate_pick)
    up = project(normed_rows, up_levels, up_scale, up_extra, up_pick)
    hidden = (jax.nn.silu(gate) * up).astype(jnp.bfloat16)
    mixed = lax.dynamic_slice_in_dim(mixed_all, lax.axis_index("tensor") * own_rows, own_rows, 0)
    down = lax.psum_scatter(
        project(hidden, down_levels, down_scale, down_extra, down_pick),
        "tensor",
        scatter_dimension=0,
        tiled=True,
    )
    return (mixed + down).astype(jnp.bfloat16)


def solution(mesh):
    placed = (
        P(("groups", "seq"), "tensor"),
        P(("groups", "seq", "tensor"), None),
        P("tensor", None),
        P(),
        P(),
        P(None, "tensor"),
        P("tensor"),
        P("tensor", None),
        P(None, "tensor"),
        P(None, "tensor"),
        P("tensor"),
        P("tensor", None),
        P(None, "tensor"),
        P("tensor", None),
        P(),
        P("tensor", None),
        P("tensor", None),
    )
    size = mesh.shape["tensor"]
    few = 4 <= size <= 8 and size & (size - 1) == 0

    def local(*args):
        return direct(size, *args) if few else plain(*args)

    return jax.shard_map(
        local,
        mesh=mesh,
        in_specs=placed,
        out_specs=P(("groups", "seq", "tensor"), None),
        check_vma=False,
    )
```

```python
import jax
import jax.numpy as jnp
from jax import lax
from jax.experimental import pallas as pl
from jax.experimental.pallas import tpu as pltpu
from jax.sharding import PartitionSpec as P


VMEM = pl.BlockSpec(memory_space=pltpu.VMEM)
SMEM = pl.BlockSpec(memory_space=pltpu.SMEM)
HBM = pl.BlockSpec(memory_space=pltpu.HBM)
ANY = pl.BlockSpec(memory_space=pl.ANY)
EPS = 1e-05
LANES = 128
COVER_FLOPS = 10**12
MLP_MIB = 14
DEPTH = 512
PART = 512
SLOTS = 6
LEAD = 1


def params(mib):
    return pltpu.CompilerParams(vmem_limit_bytes=mib * 1024 * 1024)


def whole_parts(size, want):
    for count in range(want, 0, -1):
        if size % (count * LANES) == 0:
            return count
    return 1


def chunk_of(size, want):
    return size // whole_parts(size, want)


def piece_shapes(rows, width, pieces):
    kinds = (jnp.float32, jnp.bfloat16)
    return [jax.ShapeDtypeStruct((rows, width), kinds[k % 2]) for k in range(pieces)]


def proj_kernel(rows, parts, me_ref, heads_hbm, levels_hbm, scale_hbm, stream_hbm, gain_hbm, *refs):
    stream_ref, gain_ref = refs[:2]
    outs, (heads_ref, scale_ref, held, sems) = refs[2:-4], refs[-4:]
    pieces = len(outs)
    width = levels_hbm.shape[1] // parts

    def copy(i):
        return pltpu.make_async_copy(
            levels_hbm.at[:, pl.ds(i * width, width)], held.at[i], sems.at[i]
        )

    small = [
        pltpu.make_async_copy(source, target, sems.at[parts + n])
        for n, (source, target) in enumerate((
            (heads_hbm, heads_ref), (scale_hbm, scale_ref), (stream_hbm, stream_ref), (gain_hbm, gain_ref),
        ))
    ]
    small[0].start()
    small[1].start()
    for i in range(parts):
        copy(i).start()
    small[2].start()
    small[3].start()
    me = me_ref[0]
    tokens = pieces * rows
    line = lax.broadcasted_iota(jnp.int32, (tokens, tokens), 0)
    source = jnp.bitwise_xor(lax.div(line, rows), me) * rows + lax.rem(line, rows)
    moved = lax.broadcasted_iota(jnp.int32, (tokens, tokens), 1) == source
    moved = moved.astype(jnp.float32).astype(jnp.bfloat16)
    small[0].wait()
    lhs = jnp.dot(moved, heads_ref[...], preferred_element_type=jnp.float32).astype(jnp.bfloat16)
    small[1].wait()
    for i in range(parts):
        copy(i).wait()
        cols = slice(i * width, (i + 1) * width)
        partial = jnp.dot(lhs, held[i], preferred_element_type=jnp.float32)
        partial = partial * scale_ref[:, cols]
        for k in range(pieces):
            outs[k][:, cols] = partial[k * rows : (k + 1) * rows, :].astype(outs[k].dtype)
    small[2].wait()
    small[3].wait()


def project_out(me, heads, levels, scale, stream, gain, pieces):
    features, width = levels.shape
    rows = stream.shape[0]
    parts = whole_parts(width, 8)
    shapes = [jax.ShapeDtypeStruct(a.shape, a.dtype) for a in (stream, gain)]
    shapes += piece_shapes(rows, width, pieces)

    def body(*refs):
        proj_kernel(rows, parts, *refs)

    return pl.pallas_call(
        body,
        name="project_out",
        out_shape=shapes,
        in_specs=[SMEM] + [HBM] * 5,
        out_specs=[VMEM] * (pieces + 2),
        scratch_shapes=[
            pltpu.VMEM(heads.shape, heads.dtype),
            pltpu.VMEM(scale.shape, scale.dtype),
            pltpu.VMEM((parts, features, width // parts), jnp.bfloat16),
            pltpu.SemaphoreType.DMA((parts + 4,)),
        ],
        compiler_params=params(50),
    )(me, *[pltpu.with_memory_space_constraint(a, pltpu.HBM) for a in (heads, levels, scale, stream, gain)])


def norm_kernel(after_ref, stream_ref, gain_ref, own_ref, *refs):
    del after_ref
    others, (mixed_ref, normed_ref) = refs[:-2], refs[-2:]
    mixed = own_ref[...]
    for other in others:
        mixed = mixed + other[...].astype(jnp.float32)
    mixed = stream_ref[...].astype(jnp.float32) + mixed
    mixed_ref[...] = mixed
    mean_sq = jnp.mean(mixed * mixed, axis=-1, keepdims=True)
    normed_ref[...] = (mixed * lax.rsqrt(mean_sq + EPS) * gain_ref[...]).astype(jnp.bfloat16)


def mix_and_norm(after, stream, gain, own, others):
    return pl.pallas_call(
        norm_kernel,
        name="mix_and_norm",
        out_shape=[
            jax.ShapeDtypeStruct(own.shape, jnp.float32),
            jax.ShapeDtypeStruct(own.shape, jnp.bfloat16),
        ],
        in_specs=[ANY] + [VMEM] * (3 + len(others)),
        out_specs=[VMEM] * 2,
        cost_estimate=pl.CostEstimate(flops=COVER_FLOPS, transcendentals=0, bytes_accessed=0),
        compiler_params=params(2),
    )(after, stream, gain, own, *others)


def preload(levels, columns):
    depth = levels.shape[0]
    step = columns // whole_parts(columns, 8)

    def body(levels_hbm, held, sems):
        copies = [
            pltpu.make_async_copy(
                levels_hbm.at[:, pl.ds(first, step)], held.at[:, pl.ds(first, step)], sems.at[first // step]
            )
            for first in range(0, columns, step)
        ]
        for copy in copies:
            copy.start()
        for copy in copies:
            copy.wait()

    held = pl.pallas_call(
        body,
        name="preload",
        out_shape=jax.ShapeDtypeStruct((depth, columns), levels.dtype),
        in_specs=[HBM],
        out_specs=VMEM,
        scratch_shapes=[pltpu.SemaphoreType.DMA((columns // step,))],
        cost_estimate=pl.CostEstimate(flops=10**10, transcendentals=0, bytes_accessed=0),
        compiler_params=params(1),
    )(pltpu.with_memory_space_constraint(levels, pltpu.HBM))
    return pltpu.with_memory_space_constraint(held, pltpu.VMEM)


def early_columns(levels):
    shard, width = levels.shape
    return width - (3 * width // 4) // shard * shard


def against(rows_in, extra):
    return lax.dot_general(
        rows_in, extra, (((1,), (1,)), ((), ())), preferred_element_type=jnp.float32
    )


def halves(added):
    high = added.astype(jnp.bfloat16).astype(jnp.float32)
    return jnp.concatenate([high, added - high], axis=1).astype(jnp.bfloat16)


def place(split, index_ref, first, width):
    count = split.shape[1]
    columns = lax.broadcasted_iota(jnp.int32, (count, width), 1) + first
    which = lax.broadcasted_iota(jnp.int32, (count, 1), 0)
    target = jnp.zeros((count, 1), jnp.int32)
    for k in range(count):
        target = jnp.where(which == k, index_ref[0, k % (count // 2)], target)
    chosen = (columns == target).astype(jnp.float32).astype(jnp.bfloat16)
    return jnp.dot(split, chosen, preferred_element_type=jnp.float32)


def mlp_kernel(
    rows, depth, part, lead,
    gate_scale, gate_index, gate_extra, up_scale, up_index, up_extra,
    down_scale, down_index, down_extra, gate_ref, first_ref, up_hbm, down_hbm, *refs,
):
    (x_ref, hidden_ref, gate_acc, up_acc, ring, ring_sems) = refs[-6:]
    refs = refs[:-6]
    pieces = len(refs) // 2
    ins, outs = refs[:pieces], refs[pieces:]
    slots = ring.shape[0]
    ready = first_ref.shape[1]
    shard = gate_acc.shape[1]
    steps = up_hbm.shape[0] // depth
    groups = (down_hbm.shape[1] - ready) // shard

    blocks = [(up_hbm.at[pl.ds(i * depth, depth), :], depth) for i in range(steps)]
    for c in range(groups):
        for first in range(0, shard, depth):
            count = min(depth, shard - first)
            source = down_hbm.at[pl.ds(first, count), pl.ds(ready + c * shard, shard)]
            blocks.append((source, count))

    def copies(i):
        source, count = blocks[i]
        return [
            pltpu.make_async_copy(
                source.at[pl.ds(n, min(part, count - n)), :],
                ring.at[i % slots, pl.ds(n, min(part, count - n)), :],
                ring_sems.at[i % slots, n // part],
            )
            for n in range(0, count, part)
        ]

    def start(i):
        if i < len(blocks):
            for copy in copies(i):
                copy.start()

    def arrive(i):
        for copy in copies(i):
            copy.wait()
        return ring[i % slots, : blocks[i][1], :]

    for i in range(slots):
        start(i)
    span = chunk_of(x_ref.shape[1], 8)
    for first in range(0, x_ref.shape[1], span):
        cols = slice(first, first + span)
        stacked = jnp.concatenate([piece[:, cols].astype(jnp.float32) for piece in ins], axis=0)
        x_ref[:, cols] = stacked.astype(jnp.bfloat16)

    def add(acc, s, weights):
        product = jnp.dot(
            x_ref[:, s * depth : (s + 1) * depth], weights, preferred_element_type=jnp.float32
        )
        acc[...] = product if s == 0 else acc[...] + product

    for s in range(lead + steps):
        i = s - lead
        weights = arrive(i) if i >= 0 else None
        if s < steps:
            add(gate_acc, s, gate_ref[s * depth : (s + 1) * depth, :])
        if i >= 0:
            add(up_acc, i, weights)
            start(i + slots)
    x = x_ref[...]
    count = gate_extra.shape[0]
    extras = jnp.concatenate([gate_extra[...].astype(jnp.float32), up_extra[...].astype(jnp.float32)], axis=0)
    added = against(x, extras.astype(jnp.bfloat16))
    gate_more = place(halves(added[:, :count]), gate_index, 0, shard)
    up_more = place(halves(added[:, count:]), up_index, 0, shard)
    gate = gate_acc[...] * gate_scale[...].reshape(1, shard) + gate_more
    up = up_acc[...] * up_scale[...].reshape(1, shard) + up_more
    hidden_ref[...] = (gate / (1.0 + jnp.exp(-gate)) * up).astype(jnp.bfloat16)
    hidden = hidden_ref[...]
    split = halves(against(hidden, down_extra[...]))

    def leave(total, first, count):
        cols = slice(first, first + count)
        total = total * down_scale[:, cols] + place(split, down_index, first, count)
        for k in range(pieces):
            outs[k][:, cols] = total[k * rows : (k + 1) * rows, :].astype(outs[k].dtype)

    span = chunk_of(ready, 2)
    for first in range(0, ready, span):
        leave(
            jnp.dot(hidden, first_ref[:, first : first + span], preferred_element_type=jnp.float32),
            first, span,
        )
    i = steps
    for c in range(groups):
        total = None
        for first in range(0, shard, depth):
            count = blocks[i][1]
            product = jnp.dot(
                hidden_ref[:, first : first + count], arrive(i), preferred_element_type=jnp.float32
            )
            total = product if total is None else total + product
            start(i + slots)
            i += 1
        leave(total, ready + c * shard, shard)


def mlp(normed, gate, up, down):
    gate_levels, gate_scale, gate_index, gate_extra = gate
    up_levels, up_scale, up_index, up_extra = up
    down_first, down_levels, down_scale, down_index, down_extra = down
    pieces, (rows, width) = len(normed), normed[0].shape
    shard = gate_levels.shape[1]
    tokens = pieces * rows
    shapes = piece_shapes(rows, width, pieces)

    def body(*refs):
        mlp_kernel(rows, DEPTH, PART, LEAD, *refs)

    small = [gate_scale, gate_extra.T, up_scale, up_extra.T, down_scale[None], down_extra.T]
    return pl.pallas_call(
        body,
        name="mlp",
        out_shape=shapes,
        in_specs=[VMEM, SMEM, VMEM] * 3 + [VMEM, VMEM, HBM, HBM] + [VMEM] * pieces,
        out_specs=[VMEM] * pieces,
        scratch_shapes=[
            pltpu.VMEM((tokens, width), jnp.bfloat16),
            pltpu.VMEM((tokens, shard), jnp.bfloat16),
            pltpu.VMEM((tokens, shard), jnp.float32),
            pltpu.VMEM((tokens, shard), jnp.float32),
            pltpu.VMEM((SLOTS, DEPTH, shard), jnp.bfloat16),
            pltpu.SemaphoreType.DMA((SLOTS, DEPTH // PART)),
        ],
        compiler_params=params(MLP_MIB),
    )(
        small[0], gate_index, small[1], small[2], up_index, small[3],
        small[4], down_index, small[5], gate_levels, down_first, up_levels, down_levels, *normed,
    )


def finish_kernel(mixed_ref, own_ref, *refs):
    others, out_ref = refs[:-1], refs[-1]
    down = own_ref[...]
    for other in others:
        down = down + other[...].astype(jnp.float32)
    out_ref[...] = (mixed_ref[...] + down).astype(jnp.bfloat16)


def finish(mixed, own, others):
    return pl.pallas_call(
        finish_kernel,
        name="finish",
        out_shape=jax.ShapeDtypeStruct(own.shape, jnp.bfloat16),
        in_specs=[VMEM] * (2 + len(others)),
        out_specs=VMEM,
        compiler_params=params(2),
    )(mixed, own, *others)


def moved(array, k, size):
    return lax.ppermute(array, "tensor", [(i, i ^ k) for i in range(size)])


def merge_kernel(kept_ref, passed_ref, out_ref):
    out_ref[...] = (kept_ref[...] + passed_ref[...].astype(jnp.float32)).astype(out_ref.dtype)


def merge(kept, passed):
    return pl.pallas_call(
        merge_kernel,
        name="merge",
        out_shape=jax.ShapeDtypeStruct(kept.shape, passed.dtype),
        in_specs=[VMEM] * 2,
        out_specs=VMEM,
        compiler_params=params(1),
    )(kept, passed)


def scatter(pieces, size):
    passed = {k ^ 1: moved(pieces[k], 1, size) for k in range(size - 1, 0, -2)}
    far = range(size - 2, 0, -2)
    return pieces[0], [passed[0]] + [moved(merge(pieces[k], passed[k]), k, size) for k in far]


def gather(piece, size):
    pieces = [piece] + [moved(piece, k, size) for k in range(2, size, 2)]
    passed = [moved(near, 1, size) for near in pieces]
    return [one for pair in zip(pieces, passed) for one in pair]


def direct(
    size, heads_out, stream_in, proj_levels, proj_scale, norm_gain,
    gate_levels, gate_scale, gate_index, gate_extra,
    up_levels, up_scale, up_index, up_extra,
    down_levels, down_scale, down_index, down_extra,
):
    me = lax.axis_index("tensor").astype(jnp.int32).reshape(1)
    stream, gain, *terms = project_out(
        me, heads_out, proj_levels, proj_scale[None], stream_in, norm_gain[None], size
    )
    down_first = preload(down_levels, early_columns(down_levels))
    gate_levels = pltpu.with_memory_space_constraint(gate_levels, pltpu.VMEM)
    mixed, normed = mix_and_norm(down_first, stream, gain, *scatter(terms, size))
    gathered = gather(normed, size)
    terms = mlp(
        gathered,
        (gate_levels, gate_scale, gate_index, gate_extra),
        (up_levels, up_scale, up_index, up_extra),
        (down_first, down_levels, down_scale, down_index, down_extra),
    )
    return finish(mixed, *scatter(terms, size))


def rms_norm(mixed, norm_gain):
    mean_sq = jnp.mean(mixed * mixed, axis=-1, keepdims=True)
    return (mixed * lax.rsqrt(mean_sq + EPS) * norm_gain).astype(jnp.bfloat16)


def picker(index_row, width):
    return (index_row[:, None] == jnp.arange(width, dtype=jnp.int32)[None, :]).astype(jnp.float32)


def project(rows_in, levels, scale, extra, chosen):
    base = jnp.dot(rows_in, levels, preferred_element_type=jnp.float32)
    added = jnp.dot(rows_in, extra, preferred_element_type=jnp.float32)
    return base * scale + jnp.dot(added, chosen, precision=lax.Precision.HIGHEST)


def plain(
    heads_out, stream_in, proj_levels, proj_scale, norm_gain,
    gate_levels, gate_scale, gate_index, gate_extra,
    up_levels, up_scale, up_index, up_extra,
    down_levels, down_scale, down_index, down_extra,
):
    own_rows = stream_in.shape[0]
    shard_width = gate_levels.shape[1]
    model_width = proj_levels.shape[1]
    gate_pick = picker(gate_index[0], shard_width)
    up_pick = picker(up_index[0], shard_width)
    down_pick = picker(down_index[0], model_width)
    total = lax.psum(
        jnp.dot(heads_out, proj_levels, preferred_element_type=jnp.float32) * proj_scale, "tensor"
    )
    stream_all = lax.all_gather(stream_in, "tensor", axis=0, tiled=True)
    mixed_all = stream_all.astype(jnp.float32) + total
    normed_rows = rms_norm(mixed_all, norm_gain)
    gate = project(normed_rows, gate_levels, gate_scale, gate_extra, gate_pick)
    up = project(normed_rows, up_levels, up_scale, up_extra, up_pick)
    hidden = (jax.nn.silu(gate) * up).astype(jnp.bfloat16)
    mixed = lax.dynamic_slice_in_dim(mixed_all, lax.axis_index("tensor") * own_rows, own_rows, 0)
    down = lax.psum_scatter(
        project(hidden, down_levels, down_scale, down_extra, down_pick),
        "tensor",
        scatter_dimension=0,
        tiled=True,
    )
    return (mixed + down).astype(jnp.bfloat16)


def solution(mesh):
    placed = (
        P(("groups", "seq"), "tensor"),
        P(("groups", "seq", "tensor"), None),
        P("tensor", None),
        P(),
        P(),
        P(None, "tensor"),
        P("tensor"),
        P("tensor", None),
        P(None, "tensor"),
        P(None, "tensor"),
        P("tensor"),
        P("tensor", None),
        P(None, "tensor"),
        P("tensor", None),
        P(),
        P("tensor", None),
        P("tensor", None),
    )
    size = mesh.shape["tensor"]
    few = 4 <= size <= 8 and size & (size - 1) == 0

    def local(*args):
        return direct(size, *args) if few else plain(*args)

    return jax.shard_map(
        local,
        mesh=mesh,
        in_specs=placed,
        out_specs=P(("groups", "seq", "tensor"), None),
        check_vma=False,
    )
```
